32 devices in a mesh: grp: 4 (over z), shard: 8 (over y, x, core).
Axes of the slice: x: 2, y: 2, z: 4, core: 2. Of those that a mesh axis runs over, the one named last changes fastest.
Arguments:
- latents: bfloat16 [4096, 1024], P(('grp', 'shard')), may hold values from -6 to 6
- head_weight: bfloat16 [1024, 1024], P('shard'), may hold values from -0.1875 to 0.1875
- norm_gain: float32 [1024], replicated, may hold values from 0.1 to 1.9
- color_head: bfloat16 [4, 256], replicated, may hold values from -1.5 to 1.5
- sample_points: float32 [2048, 192], P(('grp', 'shard')), may hold values from -1 to 1
- sample_spacing: float32 [2048, 64], P(('grp', 'shard')), may hold values from 0.002 to 0.02
- ray_targets: float32 [3, 2048], P(None, ('grp', 'shard')), may hold values from 0 to 1
- ray_scene: int32 [2048], P(('grp', 'shard')), may hold values from 0 to 31, as said below
Outputs:
- rendered_color: float32 [3, 2048], P(None, ('grp', 'shard'))
- loss: float32 [], replicated
- head_grad: float32 [1024, 1024], P('shard')
- norm_gain_grad: float32 [1024], replicated
- latent_grad: bfloat16 [4096, 1024], P(('grp', 'shard'))
The draws below stay inside these ranges and needn't reach their ends.
Inputs may be any that keep to these rules, and one draw needn't show every extreme that they name: `ray_scene`: one scene, drawn from the seed, is named by exactly 8 rays of every device; no device names any scene more than 8 times; every scene is named by one ray or more, and the totals of the other scenes differ from one another by one at most.
All inputs are finite; a program needn't handle non-finite values.
Results may differ from the reference program's by a relative error of at most 0.017.
Values may be sent and summed in bfloat16 or wider, within the bound.
A program may use at most 64 MiB of HBM per device.

```python
import math
import jax
import jax.numpy as jnp
from jax import lax

D = 1024
WF = 256
LAYERS = 2
RS = 64
RAY_DEV = 64
LAT = 128
SCENES = 32
RAYS = 2048
DEVICES = 32


def draw_ray_scene(key, part):
    key_hot, key_rest, key_turn, key_place = jax.random.split(jax.random.fold_in(key, 11), 4)
    hot_scene = jax.random.randint(key_hot, (), 0, SCENES)
    others = jax.random.permutation(key_rest, SCENES - 1).astype(jnp.int32)
    others = others + (others >= hot_scene).astype(jnp.int32)
    offset_turn = jax.random.randint(key_turn, (), 0, SCENES - 1)
    places = jax.random.split(key_place, DEVICES)
    shuffled = jax.vmap(lambda place_key: jax.random.permutation(place_key, RAY_DEV))(places)
    ray_rank = jnp.argsort(shuffled, axis=1, stable=True).astype(jnp.int32)
    per_device = 4 * RAY_DEV // DEVICES
    device_ids = jnp.arange(DEVICES, dtype=jnp.int32)[:, None]
    position = jnp.remainder(offset_turn + device_ids * (RAY_DEV - per_device) + ray_rank - per_device, SCENES - 1)
    scene_ids = jnp.where(ray_rank < per_device, hot_scene, others[position])
    return scene_ids.reshape(RAYS).astype(jnp.int32)


def strengthened(array, stream_key, source, target, blocks, factor):
    def block_of(axis_at):
        return (jnp.arange(array.shape[axis_at]) // (array.shape[axis_at] // blocks)).reshape((-1,) + (1,) * (array.ndim - 1 - axis_at))

    one_side = jax.random.permutation(stream_key, blocks)[block_of(target)]
    other_side = (block_of(target) + blocks // 2) % blocks
    return jnp.where((block_of(source) == one_side) | (block_of(source) == other_side), factor * array, array)


def shard_levels(stream_key, shape, shards, low, largest):
    loudness = 1.0
    for axis_at, shards_of in shards:
        steps = jax.random.uniform(jax.random.fold_in(jax.random.fold_in(stream_key, 6), axis_at), (shards_of,), jnp.float32, low / len(shards), largest / len(shards))
        loudness = loudness * jnp.repeat(jnp.exp(steps), shape[axis_at] // shards_of).reshape((-1,) + (1,) * (len(shape) - 1 - axis_at))
    return loudness


def gaussian(own_key, shape, spread, bound, cuts=(), held_as=jnp.bfloat16):
    factor_of = shard_levels(own_key, shape, cuts, -0.22, 0.18) if cuts else 1.0
    result = jax.random.normal(own_key, shape, jnp.float32) * spread * factor_of
    return jnp.minimum(jnp.maximum(result, -bound), bound).astype(held_as)


def noise_with(rng, shape, scale, bound, pieces, heavy, kind=jnp.bfloat16):
    array = scale * jax.random.normal(rng, shape, jnp.float32)
    if pieces:
        array = array * shard_levels(rng, shape, pieces, -0.22, 0.18)
    return jnp.clip(strengthened(array, jax.random.fold_in(rng, 3), *heavy), -bound, bound).astype(kind)


def setup_inputs(seed: int = 0) -> dict:
    key_list = jax.random.split(jax.random.key(seed), 9)
    return {
        "latents": noise_with(key_list[0], (SCENES * LAT, D), 1.0, 6.0, ((0, 32),), (0, 1, 32, 2.75)),
        "head_weight": gaussian(key_list[1], (D, D), D ** -0.5, 0.1875, ((0, 8),)),
        "norm_gain": jnp.clip(1.0 + 0.18 * jax.random.normal(key_list[2], (D,), jnp.float32), 0.1, 1.9),
        "color_head": gaussian(key_list[3], (4, WF), (WF // 16) ** -0.5, 1.5),
        "sample_points": jnp.clip(jax.random.uniform(key_list[4], (RAYS, 3 * RS), jnp.float32, -1.0, 1.0) * shard_levels(key_list[4], (RAYS, 3 * RS), ((0, 32),), -0.4, 0.0), -1.0, 1.0),
        "sample_spacing": jnp.clip(jnp.exp(math.log(0.02) - 2.30258502 * jax.random.uniform(key_list[5], (RAYS, RS), jnp.float32) ** shard_levels(key_list[5], (RAYS, RS), ((0, 32),), -0.2, 0.2)), 0.002, 0.02),
        "ray_targets": jnp.clip(1.0 * jax.random.uniform(key_list[6], (3, RAYS), jnp.float32) ** shard_levels(key_list[6], (3, RAYS), ((1, 32),), -0.2, 0.2), 0.0, 1.0),
        "ray_scene": draw_ray_scene(jax.random.fold_in(key_list[8], 71), 0),
    }


norm_eps = 1e-06

def encode(sample_rows, field_width):
    column = jnp.arange(field_width)
    component = column % 3
    octave = (column // 6 % 8).astype(jnp.float32)
    frequency = jnp.exp2(octave) * math.pi
    phase_shift = (column // 3 % 2).astype(jnp.float32) * (0.5 * math.pi)
    picked = jnp.zeros((sample_rows.shape[0], field_width), jnp.float32)
    for coord in range(3):
        chosen = (component == coord).astype(jnp.float32)
        picked = picked + sample_rows[:, coord:coord + 1] * chosen[None, :]
    return jnp.sin(picked * frequency + phase_shift)

def point_rows(points, ray_depth):
    ray_number = points.shape[0]
    return points.reshape(ray_number, 3, ray_depth).transpose(0, 2, 1).reshape(ray_number * ray_depth, 3)

def render_rays(points, spacing, target, live_rays, scene_factor, w_first, w_second, color_head):
    ray_number, ray_depth = spacing.shape
    field_width = w_first.shape[0]
    fan_scale = field_width ** (-0.5)
    sample_rows = point_rows(points, ray_depth)
    h_zero = encode(sample_rows, field_width).astype(jnp.bfloat16)
    h_one = jax.nn.relu(jnp.dot(h_zero, w_first, preferred_element_type=jnp.float32) * fan_scale).astype(jnp.bfloat16)
    h_two = jax.nn.relu(jnp.dot(h_one, w_second, preferred_element_type=jnp.float32) * fan_scale).astype(jnp.bfloat16)
    raw_out = lax.dot_general(color_head, h_two, (((1,), (1,)), ((), ())), preferred_element_type=jnp.float32)
    density = jax.nn.softplus(raw_out[0]).reshape(ray_number, ray_depth)
    albedo = jax.nn.sigmoid(raw_out[1:4]).reshape(3, ray_number, ray_depth)
    optical = density * spacing
    optical_before = jnp.cumsum(optical, axis=1) - optical
    transmit = jnp.exp(-optical_before)
    survive = jnp.exp(-optical)
    blend = transmit * (1.0 - survive)
    ray_color = lax.optimization_barrier(jnp.sum(blend[None] * (albedo - 1.0), axis=2)) + 1.0
    residual = ray_color - target.T
    loss_part = jnp.sum(jnp.where(live_rays, lax.optimization_barrier(jnp.sum(residual * residual, axis=0)) * scene_factor, 0.0))
    grad_color = jnp.where(live_rays[None, :], 2.0 * residual * scene_factor, 0.0)
    d_albedo = grad_color[:, :, None] * blend[None]
    d_blend = lax.optimization_barrier(jnp.sum(grad_color[:, :, None] * (albedo - 1.0), axis=0))
    weighted = d_blend * blend
    behind = lax.optimization_barrier(jnp.sum(weighted, axis=1, keepdims=True)) - jnp.cumsum(weighted, axis=1)
    d_optical = d_blend * transmit * survive - behind
    d_density = (d_optical * spacing * jax.nn.sigmoid(raw_out[0]).reshape(ray_number, ray_depth)).reshape(1, ray_number * ray_depth)
    d_tint = (d_albedo * albedo * (1.0 - albedo)).reshape(3, ray_number * ray_depth)
    d_raw = jnp.concatenate([d_density, d_tint], axis=0).astype(jnp.bfloat16)
    d_htwo = lax.dot_general(d_raw, color_head, (((0,), (0,)), ((), ())), preferred_element_type=jnp.float32)
    d_atwo = (jnp.where(h_two > 0, d_htwo, 0.0) * fan_scale).astype(jnp.bfloat16)
    grad_second = lax.dot_general(h_one, d_atwo, (((0,), (0,)), ((), ())), preferred_element_type=jnp.float32)
    d_hone = lax.dot_general(d_atwo, w_second, (((1,), (1,)), ((), ())), preferred_element_type=jnp.float32)
    d_aone = (jnp.where(h_one > 0, d_hone, 0.0) * fan_scale).astype(jnp.bfloat16)
    grad_first = lax.dot_general(h_zero, d_aone, (((0,), (0,)), ((), ())), preferred_element_type=jnp.float32)
    return (ray_color, loss_part, grad_first, grad_second)

def reference(latents, head_weight, norm_gain, color_head, sample_points, sample_spacing, ray_targets, ray_scene):
    field_width = color_head.shape[1]
    ray_total, ray_depth = sample_spacing.shape
    latent_f32 = latents.astype(jnp.float32)
    inv_rms = lax.rsqrt(lax.optimization_barrier(jnp.mean(latent_f32 * latent_f32, axis=1, keepdims=True)) + norm_eps)
    x_hat = latent_f32 * inv_rms
    x_norm = (x_hat * norm_gain).astype(jnp.bfloat16)
    field_rows = jnp.dot(x_norm, head_weight, preferred_element_type=jnp.float32).astype(jnp.bfloat16)
    field_layers = field_rows.reshape(SCENES, LAYERS, field_width, field_width)
    scene_ids = jnp.arange(SCENES, dtype=jnp.int32)
    counts = lax.optimization_barrier(jnp.sum((ray_scene[:, None] == scene_ids[None, :]).astype(jnp.int32), axis=0))
    offsets = (jnp.cumsum(counts) - counts).astype(jnp.int32)
    sort_order = jnp.argsort(ray_scene, stable=True)
    inverse = jnp.argsort(sort_order, stable=True)
    sub_rays = RAY_DEV
    points_sorted = jnp.concatenate([sample_points[sort_order], jnp.zeros((sub_rays, sample_points.shape[1]), jnp.float32)], axis=0)
    spacing_sorted = jnp.concatenate([sample_spacing[sort_order], jnp.zeros((sub_rays, ray_depth), jnp.float32)], axis=0)
    target_sorted = jnp.concatenate([ray_targets.T[sort_order], jnp.zeros((sub_rays, 3), jnp.float32)], axis=0)

    def per_scene(running, scene_item):
        colors, loss_sum = running
        weights_pair, scene_rays, offset = scene_item
        scene_factor = 1.0 / (SCENES * scene_rays.astype(jnp.float32))
        w_first = weights_pair[0]
        w_second = weights_pair[1]

        def per_block(block_index, inner):
            grad_first, grad_second, colors, loss_sum = inner
            first_row = (offset + block_index * sub_rays).astype(jnp.int32)
            points = lax.dynamic_slice_in_dim(points_sorted, first_row, sub_rays, 0)
            spacing = lax.dynamic_slice_in_dim(spacing_sorted, first_row, sub_rays, 0)
            target = lax.dynamic_slice_in_dim(target_sorted, first_row, sub_rays, 0)
            live_rays = block_index * sub_rays + jnp.arange(sub_rays, dtype=jnp.int32) < scene_rays
            ray_color, loss_part, more_first, more_second = render_rays(points, spacing, target, live_rays, scene_factor, w_first, w_second, color_head)
            previous = lax.dynamic_slice_in_dim(colors, first_row, sub_rays, 1)
            colors = lax.dynamic_update_slice_in_dim(colors, jnp.where(live_rays[None, :], ray_color, previous), first_row, 1)
            return (grad_first + more_first, grad_second + more_second, colors, loss_sum + loss_part)
        zero_grad = jnp.zeros((field_width, field_width), jnp.float32)
        block_count = ((scene_rays + sub_rays - 1) // sub_rays).astype(jnp.int32)
        grad_first, grad_second, colors, loss_sum = lax.fori_loop(jnp.int32(0), block_count, per_block, (zero_grad, zero_grad, colors, loss_sum))
        return ((colors, loss_sum), jnp.stack([grad_first, grad_second]))
    start_colors = jnp.zeros((3, ray_total + sub_rays), jnp.float32)
    (colors, loss_sum), grad_layers = lax.scan(per_scene, (start_colors, jnp.zeros((), jnp.float32)), (field_layers, counts, offsets))
    rendered_color = colors[:, :ray_total][:, inverse]
    d_field = grad_layers.reshape(SCENES * LAT, D).astype(jnp.bfloat16)
    head_grad = lax.dot_general(x_norm, d_field, (((0,), (0,)), ((), ())), preferred_element_type=jnp.float32)
    d_norm = lax.dot_general(d_field, head_weight, (((1,), (1,)), ((), ())), preferred_element_type=jnp.float32)
    norm_gain_grad = lax.optimization_barrier(jnp.sum(d_norm * x_hat, axis=0))
    d_scaled = d_norm * norm_gain
    latent_grad = (inv_rms * (d_scaled - x_hat * lax.optimization_barrier(jnp.mean(d_scaled * x_hat, axis=1, keepdims=True)))).astype(jnp.bfloat16)
    return (rendered_color, loss_sum, head_grad, norm_gain_grad, latent_grad)
```

```python
import functools

import jax
import jax.numpy as jnp
from jax import lax
from jax.experimental import pallas as pl
from jax.experimental.pallas import tpu as pltpu
from jax.sharding import PartitionSpec as P

norm_eps = 1e-06


LANES = 128
SINE = (3.14159265358979, -5.16771278004997, 2.55016403987735, -0.599264529320792, 0.0821458866111282, -0.00737043094571435, 0.000466302805767613, -0.0000219153534478303)


def sine_of_pi(turns):
    whole = jnp.floor(turns + 0.5)
    rest = turns - whole
    odd = whole - 2.0 * jnp.floor(whole * 0.5)
    square = rest * rest
    value = jnp.full_like(square, SINE[-1])
    for coefficient in SINE[-2::-1]:
        value = value * square + coefficient
    return value * (rest * (1.0 - 2.0 * odd))


def ray_kernel(
    ray_depth,
    points_ref,
    spacing_ref,
    target_ref,
    factor_ref,
    first_t_ref,
    second_t_ref,
    second_ref,
    head_ref,
    head_t_ref,
    color_ref,
    loss_ref,
    grad_first_ref,
    grad_second_ref,
    raw_ref,
    draw_ref,
):
    width = second_ref.shape[0]
    fan_scale = width ** (-0.5)
    samples = points_ref.shape[1]
    chunks = samples // LANES

    @pl.when(pl.program_id(0) == 0)
    def _():
        loss_ref[...] = jnp.zeros_like(loss_ref)
        grad_first_ref[...] = jnp.zeros_like(grad_first_ref)
        grad_second_ref[...] = jnp.zeros_like(grad_second_ref)
        draw_ref[...] = jnp.zeros_like(draw_ref)

    feature = lax.broadcasted_iota(jnp.int32, (48, 1), 0)
    component = feature % 3
    scale = jnp.exp2((feature // 6 % 8).astype(jnp.float32))
    phase = (feature // 3 % 2).astype(jnp.float32) * 0.5
    picked = jnp.where(
        component == 0,
        points_ref[0:1, :],
        jnp.where(component == 1, points_ref[1:2, :], points_ref[2:3, :]),
    )
    turns = picked * scale
    turns = turns - 2.0 * jnp.floor(turns * 0.5)
    distinct = sine_of_pi(turns + phase).astype(jnp.bfloat16)
    copies = width // 48
    h_zero = jnp.concatenate([distinct] * copies + [distinct[: width - 48 * copies]], axis=0)

    def product(a, b):
        return jnp.dot(a, b, preferred_element_type=jnp.float32)

    h_one = jnp.maximum(product(first_t_ref[...], h_zero) * fan_scale, 0.0).astype(jnp.bfloat16)
    h_two = jnp.maximum(product(second_t_ref[...], h_one) * fan_scale, 0.0).astype(jnp.bfloat16)
    raw = product(head_ref[...], h_two)
    for i in range(chunks):
        for c in range(4):
            raw_ref[c, i : i + 1, :] = raw[c : c + 1, i * LANES : (i + 1) * LANES]

    row = lax.broadcasted_iota(jnp.int32, (LANES, LANES), 0)
    column = lax.broadcasted_iota(jnp.int32, (LANES, LANES), 1)
    same = row // ray_depth == column // ray_depth
    before_sum = jnp.where(jnp.logical_and(same, row < column), 1.0, 0.0)
    behind_sum = jnp.where(jnp.logical_and(same, row > column), 1.0, 0.0)
    whole_sum = jnp.where(same, 1.0, 0.0)

    def along(values, matrix):
        return jnp.dot(
            values, matrix, preferred_element_type=jnp.float32, precision=lax.Precision.HIGHEST
        )

    spacing = spacing_ref[...]
    factor = factor_ref[...]
    density_raw = raw_ref[0]
    density = jnp.maximum(density_raw, 0.0) + jnp.log1p(jnp.exp(-jnp.abs(density_raw)))
    optical = density * spacing
    transmit = jnp.exp(-along(optical, before_sum))
    survive = jnp.exp(-optical)
    blend = transmit * (1.0 - survive)
    d_blend = jnp.zeros_like(blend)
    loss = jnp.zeros_like(blend)
    tints = []
    for c in range(3):
        albedo = 1.0 / (1.0 + jnp.exp(-raw_ref[c + 1]))
        color = along(blend * (albedo - 1.0), whole_sum) + 1.0
        color_ref[c] = color
        residual = color - target_ref[c]
        loss = loss + residual * residual
        grad_color = 2.0 * residual * factor
        d_blend = d_blend + grad_color * (albedo - 1.0)
        tints.append(grad_color * blend * albedo * (1.0 - albedo))
    loss_ref[...] += loss * factor
    behind = along(d_blend * blend, behind_sum)
    d_optical = d_blend * transmit * survive - behind
    d_density = d_optical * spacing * (1.0 / (1.0 + jnp.exp(-density_raw)))
    for c, value in enumerate([d_density] + tints):
        for i in range(chunks):
            draw_ref[c : c + 1, i * LANES : (i + 1) * LANES] = value[i : i + 1, :]
    d_raw = draw_ref[...].astype(jnp.bfloat16)
    d_htwo = product(head_t_ref[...], d_raw)
    d_atwo = (jnp.where(h_two > 0, d_htwo, 0.0) * fan_scale).astype(jnp.bfloat16)
    over_samples = (((1,), (1,)), ((), ()))
    grad_second_ref[...] += lax.dot_general(
        h_one, d_atwo, over_samples, preferred_element_type=jnp.float32
    )
    d_hone = product(second_ref[...], d_atwo)
    d_aone = (jnp.where(h_one > 0, d_hone, 0.0) * fan_scale).astype(jnp.bfloat16)
    grad_first_ref[...] += lax.dot_general(
        distinct, d_aone, over_samples, preferred_element_type=jnp.float32
    )


def render_slots(points, spacing, target, factor, w_first, w_second, color_head):
    slots, ray_depth = spacing.shape
    width = w_first.shape[0]
    total = slots * ray_depth
    block = 2048
    rows = total // LANES
    block_rows = block // LANES
    flat_points = points.reshape(slots, 3, ray_depth).transpose(1, 0, 2).reshape(3, total)
    wide_target = jnp.broadcast_to(target.T[:, :, None], (3, slots, ray_depth)).reshape(3, rows, LANES)
    wide_factor = jnp.broadcast_to(factor[:, None], (slots, ray_depth)).reshape(rows, LANES)
    head = jnp.pad(color_head, ((0, 16 - color_head.shape[0]), (0, 0)))
    fixed = lambda b: (0, 0)
    color, loss, grad_distinct, grad_second = pl.pallas_call(
        functools.partial(ray_kernel, ray_depth),
        grid=(total // block,),
        in_specs=[
            pl.BlockSpec((3, block), lambda b: (0, b)),
            pl.BlockSpec((block_rows, LANES), lambda b: (b, 0)),
            pl.BlockSpec((3, block_rows, LANES), lambda b: (0, b, 0)),
            pl.BlockSpec((block_rows, LANES), lambda b: (b, 0)),
            pl.BlockSpec((width, width), fixed),
            pl.BlockSpec((width, width), fixed),
            pl.BlockSpec((width, width), fixed),
            pl.BlockSpec((16, width), fixed),
            pl.BlockSpec((width, 16), fixed),
        ],
        out_specs=[
            pl.BlockSpec((3, block_rows, LANES), lambda b: (0, b, 0)),
            pl.BlockSpec((block_rows, LANES), fixed),
            pl.BlockSpec((48, width), fixed),
            pl.BlockSpec((width, width), fixed),
        ],
        out_shape=[
            jax.ShapeDtypeStruct((3, rows, LANES), jnp.float32),
            jax.ShapeDtypeStruct((block_rows, LANES), jnp.float32),
            jax.ShapeDtypeStruct((48, width), jnp.float32),
            jax.ShapeDtypeStruct((width, width), jnp.float32),
        ],
        scratch_shapes=[
            pltpu.VMEM((4, block_rows, LANES), jnp.float32),
            pltpu.VMEM((16, block), jnp.float32),
        ],
    )(
        flat_points,
        spacing.reshape(rows, LANES),
        wide_target,
        wide_factor,
        w_first.T,
        w_second.T,
        w_second,
        head,
        head.T,
    )
    colors = color.reshape(3, slots, ray_depth)[:, :, 0]
    copies = -(-width // 48)
    grad_first = jnp.tile(grad_distinct, (copies, 1))[:width]
    return colors, jnp.sum(loss) * (1.0 / ray_depth), grad_first, grad_second


def body(
    latents,
    head_weight,
    norm_gain,
    color_head,
    sample_points,
    sample_spacing,
    ray_targets,
    ray_scene,
):
    devices = lax.axis_size(("grp", "shard"))
    ray_count, ray_depth = sample_spacing.shape
    tokens, model = latents.shape
    field_width = color_head.shape[1]
    per_layer = field_width * field_width // model
    per_device = 4 * ray_count // devices
    slot_total = per_device * devices
    latent_f32 = latents.astype(jnp.float32)
    inv_rms = lax.rsqrt(jnp.mean(latent_f32 * latent_f32, axis=1, keepdims=True) + norm_eps)
    x_hat = latent_f32 * inv_rms
    x_norm = (x_hat * norm_gain).astype(jnp.bfloat16)
    columns = x_norm
    field_sum = jnp.dot(
        columns,
        lax.all_gather(head_weight, "shard", axis=0, tiled=True),
        preferred_element_type=jnp.float32,
    )
    field_rows = field_sum.astype(jnp.bfloat16)
    w_first = field_rows[:per_layer].reshape(field_width, field_width)
    w_second = field_rows[per_layer:].reshape(field_width, field_width)
    ray_ids = jnp.arange(ray_count, dtype=jnp.int32)
    same_scene = ray_scene[:, None] == ray_scene[None, :]
    earlier = ray_ids[:, None] < ray_ids[None, :]
    ray_rank = jnp.sum(jnp.logical_and(same_scene, earlier).astype(jnp.int32), axis=0)
    slot_of_ray = ray_scene * per_device + ray_rank
    payload = jnp.concatenate(
        [sample_points, sample_spacing, ray_targets.T, jnp.ones((ray_count, 1), jnp.float32)], axis=1
    )
    send = jnp.zeros((slot_total, payload.shape[1]), jnp.float32).at[slot_of_ray].set(payload)
    received = lax.all_to_all(send, ("grp", "shard"), split_axis=0, concat_axis=0, tiled=True)
    recv_points = received[:, : 3 * ray_depth]
    recv_spacing = received[:, 3 * ray_depth : 4 * ray_depth]
    recv_target = received[:, 4 * ray_depth : 4 * ray_depth + 3]
    recv_live = received[:, 4 * ray_depth + 3]
    scene_rays = jnp.sum(recv_live)
    scene_factor = 1.0 / (devices * scene_rays)

    slot_colors, loss_sum, grad_first, grad_second = render_slots(
        recv_points,
        recv_spacing,
        recv_target,
        recv_live * scene_factor,
        w_first,
        w_second,
        color_head,
    )
    returned = lax.all_to_all(
        slot_colors, ("grp", "shard"), split_axis=1, concat_axis=1, tiled=True
    )
    rendered = returned[:, slot_of_ray]
    d_field = jnp.concatenate(
        [grad_first.reshape(per_layer, model), grad_second.reshape(per_layer, model)], axis=0
    ).astype(jnp.bfloat16)
    d_norm = lax.dot_general(
        d_field,
        lax.all_gather(head_weight, "shard", axis=0, tiled=True),
        (((1,), (1,)), ((), ())),
        preferred_element_type=jnp.float32,
    )
    columns = x_norm
    group_part = lax.psum_scatter(
        lax.dot_general(
            columns, d_field, (((0,), (0,)), ((), ())), preferred_element_type=jnp.float32
        ).astype(jnp.bfloat16),
        "shard",
        scatter_dimension=0,
        tiled=True,
    )
    head_grad = jnp.sum(lax.all_gather(group_part, "grp", axis=0).astype(jnp.float32), axis=0)
    gain_part = jnp.sum(d_norm * x_hat, axis=0)
    norm_gain_grad, loss_total = lax.psum((gain_part, loss_sum), ("grp", "shard"))
    d_scaled = d_norm * norm_gain
    latent_grad = (
        inv_rms * (d_scaled - x_hat * jnp.mean(d_scaled * x_hat, axis=1, keepdims=True))
    ).astype(jnp.bfloat16)
    return (rendered, loss_total, head_grad, norm_gain_grad, latent_grad)


def solution(mesh):
    placed = (
        P(("grp", "shard"), None),
        P("shard", None),
        P(),
        P(),
        P(("grp", "shard"), None),
        P(("grp", "shard"), None),
        P(None, ("grp", "shard")),
        P(("grp", "shard")),
    )
    return jax.shard_map(
        body,
        mesh=mesh,
        in_specs=placed,
        out_specs=(
            P(None, ("grp", "shard")),
            P(),
            P("shard", None),
            P(),
            P(("grp", "shard"), None),
        ),
        check_vma=False,
    )
```

```python
import functools

import jax
import jax.numpy as jnp
from jax import lax
from jax.experimental import pallas as pl
from jax.experimental.pallas import tpu as pltpu
from jax.sharding import PartitionSpec as P

norm_eps = 1e-06


LANES = 128
SINE = (3.14159265358979, -5.16771278004997, 2.55016403987735, -0.599264529320792, 0.0821458866111282, -0.00737043094571435, 0.000466302805767613, -0.0000219153534478303)


def sine_of_pi(turns):
    whole = jnp.floor(turns + 0.5)
    rest = turns - whole
    odd = whole - 2.0 * jnp.floor(whole * 0.5)
    square = rest * rest
    value = jnp.full_like(square, SINE[-1])
    for coefficient in SINE[-2::-1]:
        value = value * square + coefficient
    return value * (rest * (1.0 - 2.0 * odd))


def ray_kernel(
    ray_depth,
    points_ref,
    spacing_ref,
    target_ref,
    factor_ref,
    first_t_ref,
    second_t_ref,
    second_ref,
    head_ref,
    head_t_ref,
    color_ref,
    loss_ref,
    grad_first_ref,
    grad_second_ref,
    raw_ref,
    draw_ref,
):
    width = second_ref.shape[0]
    fan_scale = width ** (-0.5)
    samples = points_ref.shape[1]
    chunks = samples // LANES

    @pl.when(pl.program_id(0) == 0)
    def _():
        loss_ref[...] = jnp.zeros_like(loss_ref)
        grad_first_ref[...] = jnp.zeros_like(grad_first_ref)
        grad_second_ref[...] = jnp.zeros_like(grad_second_ref)
        draw_ref[...] = jnp.zeros_like(draw_ref)

    feature = lax.broadcasted_iota(jnp.int32, (48, 1), 0)
    component = feature % 3
    scale = jnp.exp2((feature // 6 % 8).astype(jnp.float32))
    phase = (feature // 3 % 2).astype(jnp.float32) * 0.5
    picked = jnp.where(
        component == 0,
        points_ref[0:1, :],
        jnp.where(component == 1, points_ref[1:2, :], points_ref[2:3, :]),
    )
    turns = picked * scale
    turns = turns - 2.0 * jnp.floor(turns * 0.5)
    distinct = sine_of_pi(turns + phase).astype(jnp.bfloat16)
    copies = width // 48
    h_zero = jnp.concatenate([distinct] * copies + [distinct[: width - 48 * copies]], axis=0)

    def product(a, b):
        return jnp.dot(a, b, preferred_element_type=jnp.float32)

    h_one = jnp.maximum(product(first_t_ref[...], h_zero) * fan_scale, 0.0).astype(jnp.bfloat16)
    h_two = jnp.maximum(product(second_t_ref[...], h_one) * fan_scale, 0.0).astype(jnp.bfloat16)
    raw = product(head_ref[...], h_two)
    for i in range(chunks):
        for c in range(4):
            raw_ref[c, i : i + 1, :] = raw[c : c + 1, i * LANES : (i + 1) * LANES]

    row = lax.broadcasted_iota(jnp.int32, (LANES, LANES), 0)
    column = lax.broadcasted_iota(jnp.int32, (LANES, LANES), 1)
    same = row // ray_depth == column // ray_depth
    before_sum = jnp.where(jnp.logical_and(same, row < column), 1.0, 0.0)
    behind_sum = jnp.where(jnp.logical_and(same, row > column), 1.0, 0.0)
    whole_sum = jnp.where(same, 1.0, 0.0)

    def along(values, matrix):
        return jnp.dot(
            values, matrix, preferred_element_type=jnp.float32, precision=lax.Precision.HIGHEST
        )

    spacing = spacing_ref[...]
    factor = factor_ref[...]
    density_raw = raw_ref[0]
    density = jnp.maximum(density_raw, 0.0) + jnp.log1p(jnp.exp(-jnp.abs(density_raw)))
    optical = density * spacing
    transmit = jnp.exp(-along(optical, before_sum))
    survive = jnp.exp(-optical)
    blend = transmit * (1.0 - survive)
    d_blend = jnp.zeros_like(blend)
    loss = jnp.zeros_like(blend)
    tints = []
    for c in range(3):
        albedo = 1.0 / (1.0 + jnp.exp(-raw_ref[c + 1]))
        color = along(blend * (albedo - 1.0), whole_sum) + 1.0
        color_ref[c] = color
        residual = color - target_ref[c]
        loss = loss + residual * residual
        grad_color = 2.0 * residual * factor
        d_blend = d_blend + grad_color * (albedo - 1.0)
        tints.append(grad_color * blend * albedo * (1.0 - albedo))
    loss_ref[...] += loss * factor
    behind = along(d_blend * blend, behind_sum)
    d_optical = d_blend * transmit * survive - behind
    d_density = d_optical * spacing * (1.0 / (1.0 + jnp.exp(-density_raw)))
    for c, value in enumerate([d_density] + tints):
        for i in range(chunks):
            draw_ref[c : c + 1, i * LANES : (i + 1) * LANES] = value[i : i + 1, :]
    d_raw = draw_ref[...].astype(jnp.bfloat16)
    d_htwo = product(head_t_ref[...], d_raw)
    d_atwo = (jnp.where(h_two > 0, d_htwo, 0.0) * fan_scale).astype(jnp.bfloat16)
    over_samples = (((1,), (1,)), ((), ()))
    grad_second_ref[...] += lax.dot_general(
        h_one, d_atwo, over_samples, preferred_element_type=jnp.float32
    )
    d_hone = product(second_ref[...], d_atwo)
    d_aone = (jnp.where(h_one > 0, d_hone, 0.0) * fan_scale).astype(jnp.bfloat16)
    grad_first_ref[...] += lax.dot_general(
        distinct, d_aone, over_samples, preferred_element_type=jnp.float32
    )


def render_slots(points, spacing, target, factor, w_first, w_second, color_head):
    slots, ray_depth = spacing.shape
    width = w_first.shape[0]
    total = slots * ray_depth
    block = 2048
    rows = total // LANES
    block_rows = block // LANES
    flat_points = points.reshape(slots, 3, ray_depth).transpose(1, 0, 2).reshape(3, total)
    wide_target = jnp.broadcast_to(target.T[:, :, None], (3, slots, ray_depth)).reshape(3, rows, LANES)
    wide_factor = jnp.broadcast_to(factor[:, None], (slots, ray_depth)).reshape(rows, LANES)
    head = jnp.pad(color_head, ((0, 16 - color_head.shape[0]), (0, 0)))
    fixed = lambda b: (0, 0)
    color, loss, grad_distinct, grad_second = pl.pallas_call(
        functools.partial(ray_kernel, ray_depth),
        grid=(total // block,),
        in_specs=[
            pl.BlockSpec((3, block), lambda b: (0, b)),
            pl.BlockSpec((block_rows, LANES), lambda b: (b, 0)),
            pl.BlockSpec((3, block_rows, LANES), lambda b: (0, b, 0)),
            pl.BlockSpec((block_rows, LANES), lambda b: (b, 0)),
            pl.BlockSpec((width, width), fixed),
            pl.BlockSpec((width, width), fixed),
            pl.BlockSpec((width, width), fixed),
            pl.BlockSpec((16, width), fixed),
            pl.BlockSpec((width, 16), fixed),
        ],
        out_specs=[
            pl.BlockSpec((3, block_rows, LANES), lambda b: (0, b, 0)),
            pl.BlockSpec((block_rows, LANES), fixed),
            pl.BlockSpec((48, width), fixed),
            pl.BlockSpec((width, width), fixed),
        ],
        out_shape=[
            jax.ShapeDtypeStruct((3, rows, LANES), jnp.float32),
            jax.ShapeDtypeStruct((block_rows, LANES), jnp.float32),
            jax.ShapeDtypeStruct((48, width), jnp.float32),
            jax.ShapeDtypeStruct((width, width), jnp.float32),
        ],
        scratch_shapes=[
            pltpu.VMEM((4, block_rows, LANES), jnp.float32),
            pltpu.VMEM((16, block), jnp.float32),
        ],
    )(
        flat_points,
        spacing.reshape(rows, LANES),
        wide_target,
        wide_factor,
        w_first.T,
        w_second.T,
        w_second,
        head,
        head.T,
    )
    colors = color.reshape(3, slots, ray_depth)[:, :, 0]
    copies = -(-width // 48)
    grad_first = jnp.tile(grad_distinct, (copies, 1))[:width]
    return colors, jnp.sum(loss) * (1.0 / ray_depth), grad_first, grad_second


MESH = pl.DeviceIdType.MESH


def greet_all(groups, shards):
    me = lax.axis_index("grp") * shards + lax.axis_index("shard")
    total = groups * shards
    barrier = pltpu.get_barrier_semaphore()

    def greet(step, carry):
        other = lax.rem(me + step, total)
        pl.semaphore_signal(
            barrier, inc=1, device_id=(other // shards, lax.rem(other, shards)), device_id_type=MESH
        )
        return carry

    lax.fori_loop(1, total, greet, 0)
    pl.semaphore_wait(barrier, total - 1)


def messages(groups, shards, message_ref, landed, sent, arrived):
    me = lax.axis_index("grp") * shards + lax.axis_index("shard")
    total = groups * shards

    def copy_to(step):
        other = lax.rem(me + step, total)
        return pltpu.make_async_remote_copy(
            src_ref=message_ref.at[other],
            dst_ref=landed.at[me],
            send_sem=sent.at[other],
            recv_sem=arrived.at[me],
            device_id=(other // shards, lax.rem(other, shards)),
            device_id_type=MESH,
        )

    def copy_from(step):
        other = lax.rem(me + total - step, total)
        return pltpu.make_async_remote_copy(
            src_ref=message_ref.at[other],
            dst_ref=landed.at[other],
            send_sem=sent.at[other],
            recv_sem=arrived.at[other],
            device_id=(other // shards, lax.rem(other, shards)),
            device_id_type=MESH,
        )

    def start():
        def one(step, carry):
            copy_to(step).start()
            return carry

        lax.fori_loop(1, total, one, 0)

    def finish():
        def one(step, carry):
            copy_from(step).wait_recv()
            copy_to(step).wait_send()
            return carry

        lax.fori_loop(1, total, one, 0)

    return start, finish


def tail_kernel(
    groups,
    shards,
    message_ref,
    turned_ref,
    field_ref,
    sums_ref,
    colors_ref,
    head_ref,
    landed,
    turned,
    fields,
    part,
    parts,
    done,
    message_sent,
    message_arrived,
    turned_sent,
    turned_arrived,
    field_sent,
    passed_on,
    field_arrived,
    part_sent,
    part_arrived,
    done_sent,
    done_arrived,
):
    group = lax.axis_index("grp")
    shard = lax.axis_index("shard")
    me = group * shards + shard
    chips = shards // 2
    chip = shard // 2
    core = lax.rem(shard, 2)
    partner = chip * 2 + 1 - core

    def remote(source, target, send_sem, recv_sem, to_group, to_shard):
        return pltpu.make_async_remote_copy(
            src_ref=source,
            dst_ref=target,
            send_sem=send_sem,
            recv_sem=recv_sem,
            device_id=(to_group, to_shard),
            device_id_type=MESH,
        )

    def field_to(other):
        return remote(
            field_ref, fields.at[shard], field_sent.at[other], field_arrived.at[shard], group, other
        )

    def field_pass(origin):
        return remote(
            fields.at[origin],
            fields.at[origin],
            passed_on.at[origin],
            field_arrived.at[origin],
            group,
            partner,
        )

    def turned_to(other):
        return remote(
            turned_ref.at[other],
            turned.at[shard],
            turned_sent.at[other],
            turned_arrived.at[shard],
            group,
            other,
        )

    def turned_from(other):
        return remote(
            turned_ref.at[other],
            turned.at[other],
            turned_sent.at[other],
            turned_arrived.at[other],
            group,
            other,
        )

    greet_all(groups, shards)
    start_messages, finish_messages = messages(
        groups, shards, message_ref, landed, message_sent, message_arrived
    )
    peers = [lax.rem(chip + step, chips) * 2 + core for step in range(1, chips)]
    origins = [lax.rem(chip + chips - step, chips) * 2 + core for step in range(1, chips)]
    others = [lax.rem(shard + step, shards) for step in range(1, shards)]
    for other in peers:
        field_to(other).start()
    field_to(partner).start()
    for other in others:
        turned_to(other).start()
    start_messages()

    def product(rows, field):
        return jnp.dot(rows, field, preferred_element_type=jnp.float32)

    total = product(turned_ref[shard], field_ref[...])
    field_pass(partner).wait_recv()
    turned_from(partner).wait_recv()
    total = total + product(turned[partner], fields[partner])
    for origin in origins:
        field_pass(origin).wait_recv()
        field_pass(origin).start()
        turned_from(origin).wait_recv()
        total = total + product(turned[origin], fields[origin])
    for origin in origins:
        across = origin + 1 - 2 * core
        field_pass(across).wait_recv()
        turned_from(across).wait_recv()
        total = total + product(turned[across], fields[across])

    part[...] = total.astype(jnp.bfloat16).reshape(part.shape)
    group_steps = [lax.rem(group + step, groups) for step in range(1, groups)]

    def part_to(other):
        return remote(
            part.at[other], parts.at[group], part_sent.at[other], part_arrived.at[group], other, shard
        )

    def part_from(other):
        return remote(
            part.at[other], parts.at[other], part_sent.at[other], part_arrived.at[other], other, shard
        )

    def done_to(other):
        return remote(
            done.at[group], done.at[group], done_sent.at[other], done_arrived.at[group], other, shard
        )

    def done_from(other):
        return remote(
            done.at[other], done.at[other], done_sent.at[other], done_arrived.at[other], other, shard
        )

    for other in group_steps:
        part_to(other).start()
    slice_sum = part[group].astype(jnp.float32)
    for other in group_steps:
        part_from(other).wait_recv()
        slice_sum = slice_sum + parts[other].astype(jnp.float32)
    done[group] = slice_sum.astype(jnp.bfloat16)
    for other in group_steps:
        done_to(other).start()
    head_ref[group] = slice_sum

    finish_messages()
    landed[me] = message_ref[me]
    colors_ref[...] = landed[:, landed.shape[1] - 8 :, :]
    sums_ref[...] = jnp.sum(landed[...], axis=0)

    for other in group_steps:
        done_from(other).wait_recv()
        head_ref[other] = done[other].astype(jnp.float32)
    for other in peers:
        field_to(other).wait_send()
    field_to(partner).wait_send()
    for origin in origins:
        field_pass(origin).wait_send()
    for other in others:
        turned_to(other).wait_send()
    for other in group_steps:
        part_to(other).wait_send()
        done_to(other).wait_send()


def tail_exchange(groups, shards, x_norm, d_field, gain_part, loss_sum, slot_colors):
    tokens, model = x_norm.shape
    devices = groups * shards
    rows = model // shards
    gain_rows = model // LANES
    per_device = slot_colors.shape[1] // devices
    turned = x_norm.T.reshape(shards, rows, tokens)
    shared = jnp.concatenate(
        [gain_part.reshape(gain_rows, LANES), jnp.broadcast_to(loss_sum, (1, LANES))], axis=0
    )
    own = jnp.pad(
        slot_colors.reshape(3, devices, per_device).transpose(1, 0, 2),
        ((0, 0), (0, 4), (0, LANES - per_device)),
    )
    message = jnp.concatenate(
        [jnp.broadcast_to(shared[None], (devices,) + shared.shape), own], axis=1
    )
    in_vmem = pl.BlockSpec(memory_space=pltpu.VMEM)
    dma = pltpu.SemaphoreType.DMA
    sums, colors, head = pl.pallas_call(
        functools.partial(tail_kernel, groups, shards),
        in_specs=[in_vmem] * 3,
        out_specs=[in_vmem] * 3,
        out_shape=[
            jax.ShapeDtypeStruct(message.shape[1:], jnp.float32),
            jax.ShapeDtypeStruct((devices, 8, LANES), jnp.float32),
            jax.ShapeDtypeStruct((groups, rows // groups, model), jnp.float32),
        ],
        scratch_shapes=[
            pltpu.VMEM(message.shape, jnp.float32),
            pltpu.VMEM(turned.shape, jnp.bfloat16),
            pltpu.VMEM((shards, tokens, model), jnp.bfloat16),
            pltpu.VMEM((groups, rows // groups, model), jnp.bfloat16),
            pltpu.VMEM((groups, rows // groups, model), jnp.bfloat16),
            pltpu.VMEM((groups, rows // groups, model), jnp.bfloat16),
            dma((devices,)),
            dma((devices,)),
            dma((shards,)),
            dma((shards,)),
            dma((shards,)),
            dma((shards,)),
            dma((shards,)),
            dma((groups,)),
            dma((groups,)),
            dma((groups,)),
            dma((groups,)),
        ],
        compiler_params=pltpu.CompilerParams(collective_id=1, has_side_effects=True),
    )(message, turned, d_field)
    gain = sums[:gain_rows].reshape(model)
    loss = sums[gain_rows, 0]
    returned = colors[:, 1:4, :per_device].transpose(1, 0, 2).reshape(3, devices * per_device)
    return returned, loss, head.reshape(rows, model), gain


def body(
    latents,
    head_weight,
    norm_gain,
    color_head,
    sample_points,
    sample_spacing,
    ray_targets,
    ray_scene,
):
    devices = lax.axis_size(("grp", "shard"))
    ray_count, ray_depth = sample_spacing.shape
    tokens, model = latents.shape
    field_width = color_head.shape[1]
    per_layer = field_width * field_width // model
    per_device = 4 * ray_count // devices
    slot_total = per_device * devices
    latent_f32 = latents.astype(jnp.float32)
    inv_rms = lax.rsqrt(jnp.mean(latent_f32 * latent_f32, axis=1, keepdims=True) + norm_eps)
    x_hat = latent_f32 * inv_rms
    x_norm = (x_hat * norm_gain).astype(jnp.bfloat16)
    columns = x_norm
    field_sum = jnp.dot(
        columns,
        lax.all_gather(head_weight, "shard", axis=0, tiled=True),
        preferred_element_type=jnp.float32,
    )
    field_rows = field_sum.astype(jnp.bfloat16)
    w_first = field_rows[:per_layer].reshape(field_width, field_width)
    w_second = field_rows[per_layer:].reshape(field_width, field_width)
    ray_ids = jnp.arange(ray_count, dtype=jnp.int32)
    same_scene = ray_scene[:, None] == ray_scene[None, :]
    earlier = ray_ids[:, None] < ray_ids[None, :]
    ray_rank = jnp.sum(jnp.logical_and(same_scene, earlier).astype(jnp.int32), axis=0)
    slot_of_ray = ray_scene * per_device + ray_rank
    payload = jnp.concatenate(
        [sample_points, sample_spacing, ray_targets.T, jnp.ones((ray_count, 1), jnp.float32)], axis=1
    )
    send = jnp.zeros((slot_total, payload.shape[1]), jnp.float32).at[slot_of_ray].set(payload)
    received = lax.all_to_all(send, ("grp", "shard"), split_axis=0, concat_axis=0, tiled=True)
    recv_points = received[:, : 3 * ray_depth]
    recv_spacing = received[:, 3 * ray_depth : 4 * ray_depth]
    recv_target = received[:, 4 * ray_depth : 4 * ray_depth + 3]
    recv_live = received[:, 4 * ray_depth + 3]
    scene_rays = jnp.sum(recv_live)
    scene_factor = 1.0 / (devices * scene_rays)

    slot_colors, loss_sum, grad_first, grad_second = render_slots(
        recv_points,
        recv_spacing,
        recv_target,
        recv_live * scene_factor,
        w_first,
        w_second,
        color_head,
    )
    d_field = jnp.concatenate(
        [grad_first.reshape(per_layer, model), grad_second.reshape(per_layer, model)], axis=0
    ).astype(jnp.bfloat16)
    d_norm = lax.dot_general(
        d_field,
        lax.all_gather(head_weight, "shard", axis=0, tiled=True),
        (((1,), (1,)), ((), ())),
        preferred_element_type=jnp.float32,
    )
    gain_part = jnp.sum(d_norm * x_hat, axis=0)
    returned, loss_total, head_grad, norm_gain_grad = tail_exchange(
        lax.axis_size("grp"), lax.axis_size("shard"), x_norm, d_field, gain_part, loss_sum, slot_colors
    )
    rendered = returned[:, slot_of_ray]
    d_scaled = d_norm * norm_gain
    latent_grad = (
        inv_rms * (d_scaled - x_hat * jnp.mean(d_scaled * x_hat, axis=1, keepdims=True))
    ).astype(jnp.bfloat16)
    return (rendered, loss_total, head_grad, norm_gain_grad, latent_grad)


def solution(mesh):
    placed = (
        P(("grp", "shard"), None),
        P("shard", None),
        P(),
        P(),
        P(("grp", "shard"), None),
        P(("grp", "shard"), None),
        P(None, ("grp", "shard")),
        P(("grp", "shard")),
    )
    return jax.shard_map(
        body,
        mesh=mesh,
        in_specs=placed,
        out_specs=(
            P(None, ("grp", "shard")),
            P(),
            P("shard", None),
            P(),
            P(("grp", "shard"), None),
        ),
        check_vma=False,
    )
```

```python
import functools

import jax
import jax.numpy as jnp
from jax import lax
from jax.experimental import pallas as pl
from jax.experimental.pallas import tpu as pltpu
from jax.sharding import PartitionSpec as P

norm_eps = 1e-06


LANES = 128
SINE = (3.14159265358979, -5.16771278004997, 2.55016403987735, -0.599264529320792, 0.0821458866111282, -0.00737043094571435, 0.000466302805767613, -0.0000219153534478303)


def sine_of_pi(turns):
    whole = jnp.floor(turns + 0.5)
    rest = turns - whole
    odd = whole - 2.0 * jnp.floor(whole * 0.5)
    square = rest * rest
    value = jnp.full_like(square, SINE[-1])
    for coefficient in SINE[-2::-1]:
        value = value * square + coefficient
    return value * (rest * (1.0 - 2.0 * odd))


def ray_kernel(
    ray_depth,
    points_ref,
    spacing_ref,
    target_ref,
    factor_ref,
    first_t_ref,
    second_t_ref,
    second_ref,
    head_ref,
    head_t_ref,
    color_ref,
    loss_ref,
    grad_first_ref,
    grad_second_ref,
    raw_ref,
    draw_ref,
):
    width = second_ref.shape[0]
    fan_scale = width ** (-0.5)
    samples = points_ref.shape[1]
    chunks = samples // LANES

    @pl.when(pl.program_id(0) == 0)
    def _():
        loss_ref[...] = jnp.zeros_like(loss_ref)
        grad_first_ref[...] = jnp.zeros_like(grad_first_ref)
        grad_second_ref[...] = jnp.zeros_like(grad_second_ref)
        draw_ref[...] = jnp.zeros_like(draw_ref)

    feature = lax.broadcasted_iota(jnp.int32, (48, 1), 0)
    component = feature % 3
    scale = jnp.exp2((feature // 6 % 8).astype(jnp.float32))
    phase = (feature // 3 % 2).astype(jnp.float32) * 0.5
    picked = jnp.where(
        component == 0,
        points_ref[0:1, :],
        jnp.where(component == 1, points_ref[1:2, :], points_ref[2:3, :]),
    )
    turns = picked * scale
    turns = turns - 2.0 * jnp.floor(turns * 0.5)
    distinct = sine_of_pi(turns + phase).astype(jnp.bfloat16)
    copies = width // 48
    h_zero = jnp.concatenate([distinct] * copies + [distinct[: width - 48 * copies]], axis=0)

    def product(a, b):
        return jnp.dot(a, b, preferred_element_type=jnp.float32)

    h_one = jnp.maximum(product(first_t_ref[...], h_zero) * fan_scale, 0.0).astype(jnp.bfloat16)
    h_two = jnp.maximum(product(second_t_ref[...], h_one) * fan_scale, 0.0).astype(jnp.bfloat16)
    raw = product(head_ref[...], h_two)
    for i in range(chunks):
        for c in range(4):
            raw_ref[c, i : i + 1, :] = raw[c : c + 1, i * LANES : (i + 1) * LANES]

    row = lax.broadcasted_iota(jnp.int32, (LANES, LANES), 0)
    column = lax.broadcasted_iota(jnp.int32, (LANES, LANES), 1)
    same = row // ray_depth == column // ray_depth
    before_sum = jnp.where(jnp.logical_and(same, row < column), 1.0, 0.0)
    behind_sum = jnp.where(jnp.logical_and(same, row > column), 1.0, 0.0)
    whole_sum = jnp.where(same, 1.0, 0.0)

    def along(values, matrix):
        return jnp.dot(
            values, matrix, preferred_element_type=jnp.float32, precision=lax.Precision.HIGHEST
        )

    spacing = spacing_ref[...]
    factor = factor_ref[...]
    density_raw = raw_ref[0]
    density = jnp.maximum(density_raw, 0.0) + jnp.log1p(jnp.exp(-jnp.abs(density_raw)))
    optical = density * spacing
    transmit = jnp.exp(-along(optical, before_sum))
    survive = jnp.exp(-optical)
    blend = transmit * (1.0 - survive)
    d_blend = jnp.zeros_like(blend)
    loss = jnp.zeros_like(blend)
    tints = []
    for c in range(3):
        albedo = 1.0 / (1.0 + jnp.exp(-raw_ref[c + 1]))
        color = along(blend * (albedo - 1.0), whole_sum) + 1.0
        color_ref[c] = color
        residual = color - target_ref[c]
        loss = loss + residual * residual
        grad_color = 2.0 * residual * factor
        d_blend = d_blend + grad_color * (albedo - 1.0)
        tints.append(grad_color * blend * albedo * (1.0 - albedo))
    loss_ref[...] += loss * factor
    behind = along(d_blend * blend, behind_sum)
    d_optical = d_blend * transmit * survive - behind
    d_density = d_optical * spacing * (1.0 / (1.0 + jnp.exp(-density_raw)))
    for c, value in enumerate([d_density] + tints):
        for i in range(chunks):
            draw_ref[c : c + 1, i * LANES : (i + 1) * LANES] = value[i : i + 1, :]
    d_raw = draw_ref[...].astype(jnp.bfloat16)
    d_htwo = product(head_t_ref[...], d_raw)
    d_atwo = (jnp.where(h_two > 0, d_htwo, 0.0) * fan_scale).astype(jnp.bfloat16)
    over_samples = (((1,), (1,)), ((), ()))
    grad_second_ref[...] += lax.dot_general(
        h_one, d_atwo, over_samples, preferred_element_type=jnp.float32
    )
    d_hone = product(second_ref[...], d_atwo)
    d_aone = (jnp.where(h_one > 0, d_hone, 0.0) * fan_scale).astype(jnp.bfloat16)
    grad_first_ref[...] += lax.dot_general(
        distinct, d_aone, over_samples, preferred_element_type=jnp.float32
    )


def render_slots(points, spacing, target, factor, w_first, w_second, color_head):
    slots, ray_depth = spacing.shape
    width = w_first.shape[0]
    total = slots * ray_depth
    block = 2048
    rows = total // LANES
    block_rows = block // LANES
    flat_points = points.reshape(slots, 3, ray_depth).transpose(1, 0, 2).reshape(3, total)
    wide_target = jnp.broadcast_to(target.T[:, :, None], (3, slots, ray_depth)).reshape(3, rows, LANES)
    wide_factor = jnp.broadcast_to(factor[:, None], (slots, ray_depth)).reshape(rows, LANES)
    head = jnp.pad(color_head, ((0, 16 - color_head.shape[0]), (0, 0)))
    fixed = lambda b: (0, 0)
    color, loss, grad_distinct, grad_second = pl.pallas_call(
        functools.partial(ray_kernel, ray_depth),
        grid=(total // block,),
        in_specs=[
            pl.BlockSpec((3, block), lambda b: (0, b)),
            pl.BlockSpec((block_rows, LANES), lambda b: (b, 0)),
            pl.BlockSpec((3, block_rows, LANES), lambda b: (0, b, 0)),
            pl.BlockSpec((block_rows, LANES), lambda b: (b, 0)),
            pl.BlockSpec((width, width), fixed),
            pl.BlockSpec((width, width), fixed),
            pl.BlockSpec((width, width), fixed),
            pl.BlockSpec((16, width), fixed),
            pl.BlockSpec((width, 16), fixed),
        ],
        out_specs=[
            pl.BlockSpec((3, block_rows, LANES), lambda b: (0, b, 0)),
            pl.BlockSpec((block_rows, LANES), fixed),
            pl.BlockSpec((48, width), fixed),
            pl.BlockSpec((width, width), fixed),
        ],
        out_shape=[
            jax.ShapeDtypeStruct((3, rows, LANES), jnp.float32),
            jax.ShapeDtypeStruct((block_rows, LANES), jnp.float32),
            jax.ShapeDtypeStruct((48, width), jnp.float32),
            jax.ShapeDtypeStruct((width, width), jnp.float32),
        ],
        scratch_shapes=[
            pltpu.VMEM((4, block_rows, LANES), jnp.float32),
            pltpu.VMEM((16, block), jnp.float32),
        ],
    )(
        flat_points,
        spacing.reshape(rows, LANES),
        wide_target,
        wide_factor,
        w_first.T,
        w_second.T,
        w_second,
        head,
        head.T,
    )
    colors = color.reshape(3, slots, ray_depth)[:, :, 0]
    copies = -(-width // 48)
    grad_first = jnp.tile(grad_distinct, (copies, 1))[:width]
    return colors, jnp.sum(loss) * (1.0 / ray_depth), grad_first, grad_second


MESH = pl.DeviceIdType.MESH


def greet_all(groups, shards):
    me = lax.axis_index("grp") * shards + lax.axis_index("shard")
    total = groups * shards
    barrier = pltpu.get_barrier_semaphore()

    def greet(step, carry):
        other = lax.rem(me + step, total)
        pl.semaphore_signal(
            barrier, inc=1, device_id=(other // shards, lax.rem(other, shards)), device_id_type=MESH
        )
        return carry

    lax.fori_loop(1, total, greet, 0)
    pl.semaphore_wait(barrier, total - 1)


def messages(groups, shards, message_ref, landed, sent, arrived):
    me = lax.axis_index("grp") * shards + lax.axis_index("shard")
    total = groups * shards

    def copy_to(step):
        other = lax.rem(me + step, total)
        return pltpu.make_async_remote_copy(
            src_ref=message_ref.at[other],
            dst_ref=landed.at[me],
            send_sem=sent.at[other],
            recv_sem=arrived.at[me],
            device_id=(other // shards, lax.rem(other, shards)),
            device_id_type=MESH,
        )

    def copy_from(step):
        other = lax.rem(me + total - step, total)
        return pltpu.make_async_remote_copy(
            src_ref=message_ref.at[other],
            dst_ref=landed.at[other],
            send_sem=sent.at[other],
            recv_sem=arrived.at[other],
            device_id=(other // shards, lax.rem(other, shards)),
            device_id_type=MESH,
        )

    def start():
        def one(step, carry):
            copy_to(step).start()
            return carry

        lax.fori_loop(1, total, one, 0)

    def finish():
        def one(step, carry):
            copy_from(step).wait_recv()
            copy_to(step).wait_send()
            return carry

        lax.fori_loop(1, total, one, 0)

    return start, finish


def tail_kernel(
    groups,
    shards,
    message_ref,
    turned_ref,
    field_ref,
    sums_ref,
    colors_ref,
    head_ref,
    landed,
    fields,
    part,
    parts,
    done,
    message_sent,
    message_arrived,
    field_sent,
    passed_on,
    field_arrived,
    part_sent,
    part_arrived,
    done_sent,
    done_arrived,
):
    group = lax.axis_index("grp")
    shard = lax.axis_index("shard")
    me = group * shards + shard
    chips = shards // 2
    chip = shard // 2
    core = lax.rem(shard, 2)
    partner = chip * 2 + 1 - core

    def remote(source, target, send_sem, recv_sem, to_group, to_shard):
        return pltpu.make_async_remote_copy(
            src_ref=source,
            dst_ref=target,
            send_sem=send_sem,
            recv_sem=recv_sem,
            device_id=(to_group, to_shard),
            device_id_type=MESH,
        )

    def field_to(other):
        return remote(
            field_ref, fields.at[shard], field_sent.at[other], field_arrived.at[shard], group, other
        )

    def field_pass(origin):
        return remote(
            fields.at[origin],
            fields.at[origin],
            passed_on.at[origin],
            field_arrived.at[origin],
            group,
            partner,
        )

    greet_all(groups, shards)
    start_messages, finish_messages = messages(
        groups, shards, message_ref, landed, message_sent, message_arrived
    )
    peers = [lax.rem(chip + step, chips) * 2 + core for step in range(1, chips)]
    origins = [lax.rem(chip + chips - step, chips) * 2 + core for step in range(1, chips)]
    for other in peers:
        field_to(other).start()
    field_to(partner).start()
    start_messages()

    def product(rows, field):
        return jnp.dot(rows, field, preferred_element_type=jnp.float32)

    total = product(turned_ref[shard], field_ref[...])
    field_pass(partner).wait_recv()
    total = total + product(turned_ref[partner], fields[partner])
    for origin in origins:
        field_pass(origin).wait_recv()
        field_pass(origin).start()
        total = total + product(turned_ref[origin], fields[origin])
    for origin in origins:
        across = origin + 1 - 2 * core
        field_pass(across).wait_recv()
        total = total + product(turned_ref[across], fields[across])

    part[...] = total.astype(jnp.bfloat16).reshape(part.shape)
    group_steps = [lax.rem(group + step, groups) for step in range(1, groups)]

    def part_to(other):
        return remote(
            part.at[other], parts.at[group], part_sent.at[other], part_arrived.at[group], other, shard
        )

    def part_from(other):
        return remote(
            part.at[other], parts.at[other], part_sent.at[other], part_arrived.at[other], other, shard
        )

    def done_to(other):
        return remote(
            done.at[group], done.at[group], done_sent.at[other], done_arrived.at[group], other, shard
        )

    def done_from(other):
        return remote(
            done.at[other], done.at[other], done_sent.at[other], done_arrived.at[other], other, shard
        )

    for other in group_steps:
        part_to(other).start()
    slice_sum = part[group].astype(jnp.float32)
    for other in group_steps:
        part_from(other).wait_recv()
        slice_sum = slice_sum + parts[other].astype(jnp.float32)
    done[group] = slice_sum.astype(jnp.bfloat16)
    for other in group_steps:
        done_to(other).start()
    head_ref[group] = slice_sum

    finish_messages()
    landed[me] = message_ref[me]
    colors_ref[...] = landed[:, landed.shape[1] - 8 :, :]
    sums_ref[...] = jnp.sum(landed[...], axis=0)

    for other in group_steps:
        done_from(other).wait_recv()
        head_ref[other] = done[other].astype(jnp.float32)
    for other in peers:
        field_to(other).wait_send()
    field_to(partner).wait_send()
    for origin in origins:
        field_pass(origin).wait_send()
    for other in group_steps:
        part_to(other).wait_send()
        done_to(other).wait_send()


def tail_exchange(groups, shards, turned, d_field, gain_part, loss_sum, slot_colors):
    tokens, model = d_field.shape
    devices = groups * shards
    rows = model // shards
    gain_rows = model // LANES
    per_device = slot_colors.shape[1] // devices
    shared = jnp.concatenate(
        [gain_part.reshape(gain_rows, LANES), jnp.broadcast_to(loss_sum, (1, LANES))], axis=0
    )
    own = jnp.pad(
        slot_colors.reshape(3, devices, per_device).transpose(1, 0, 2),
        ((0, 0), (0, 4), (0, LANES - per_device)),
    )
    message = jnp.concatenate(
        [jnp.broadcast_to(shared[None], (devices,) + shared.shape), own], axis=1
    )
    in_vmem = pl.BlockSpec(memory_space=pltpu.VMEM)
    dma = pltpu.SemaphoreType.DMA
    sums, colors, head = pl.pallas_call(
        functools.partial(tail_kernel, groups, shards),
        in_specs=[in_vmem] * 3,
        out_specs=[in_vmem] * 3,
        out_shape=[
            jax.ShapeDtypeStruct(message.shape[1:], jnp.float32),
            jax.ShapeDtypeStruct((devices, 8, LANES), jnp.float32),
            jax.ShapeDtypeStruct((groups, rows // groups, model), jnp.float32),
        ],
        scratch_shapes=[
            pltpu.VMEM(message.shape, jnp.float32),
            pltpu.VMEM((shards, tokens, model), jnp.bfloat16),
            pltpu.VMEM((groups, rows // groups, model), jnp.bfloat16),
            pltpu.VMEM((groups, rows // groups, model), jnp.bfloat16),
            pltpu.VMEM((groups, rows // groups, model), jnp.bfloat16),
            dma((devices,)),
            dma((devices,)),
            dma((shards,)),
            dma((shards,)),
            dma((shards,)),
            dma((groups,)),
            dma((groups,)),
            dma((groups,)),
            dma((groups,)),
        ],
        compiler_params=pltpu.CompilerParams(collective_id=1, has_side_effects=True),
    )(message, turned, d_field)
    gain = sums[:gain_rows].reshape(model)
    loss = sums[gain_rows, 0]
    returned = colors[:, 1:4, :per_device].transpose(1, 0, 2).reshape(3, devices * per_device)
    return returned, loss, head.reshape(rows, model), gain


def start_kernel(
    groups,
    shards,
    message_ref,
    turned_ref,
    weight_ref,
    received_ref,
    turned_all_ref,
    weight_all_ref,
    field_ref,
    landed,
    turned,
    weights,
    message_sent,
    message_arrived,
    turned_sent,
    turned_arrived,
    weight_sent,
    passed_on,
    weight_arrived,
):
    group = lax.axis_index("grp")
    shard = lax.axis_index("shard")
    me = group * shards + shard
    chips = shards // 2
    chip = shard // 2
    core = lax.rem(shard, 2)
    partner = chip * 2 + 1 - core

    def remote(source, target, send_sem, recv_sem, to_shard):
        return pltpu.make_async_remote_copy(
            src_ref=source,
            dst_ref=target,
            send_sem=send_sem,
            recv_sem=recv_sem,
            device_id=(group, to_shard),
            device_id_type=MESH,
        )

    def weight_to(other):
        return remote(
            weight_ref, weights.at[shard], weight_sent.at[other], weight_arrived.at[shard], other
        )

    def weight_pass(origin):
        return remote(
            weights.at[origin],
            weights.at[origin],
            passed_on.at[origin],
            weight_arrived.at[origin],
            partner,
        )

    def turned_to(other):
        return remote(
            turned_ref.at[other],
            turned.at[shard],
            turned_sent.at[other],
            turned_arrived.at[shard],
            other,
        )

    def turned_from(other):
        return remote(
            turned_ref.at[other],
            turned.at[other],
            turned_sent.at[other],
            turned_arrived.at[other],
            other,
        )

    greet_all(groups, shards)
    start_messages, finish_messages = messages(
        groups, shards, message_ref, landed, message_sent, message_arrived
    )
    peers = [lax.rem(chip + step, chips) * 2 + core for step in range(1, chips)]
    origins = [lax.rem(chip + chips - step, chips) * 2 + core for step in range(1, chips)]
    others = [lax.rem(shard + step, shards) for step in range(1, shards)]
    for other in peers:
        weight_to(other).start()
    weight_to(partner).start()
    start_messages()
    for other in others:
        turned_to(other).start()

    def product(rows, weight):
        return lax.dot_general(
            rows, weight, (((0,), (0,)), ((), ())), preferred_element_type=jnp.float32
        )

    total = product(turned_ref[shard], weight_ref[...])
    weight_all_ref[shard] = weight_ref[...]
    turned_all_ref[shard] = turned_ref[shard]
    weight_pass(partner).wait_recv()
    total = total + product(turned_ref[partner], weights[partner])
    weight_all_ref[partner] = weights[partner]
    for origin in origins:
        weight_pass(origin).wait_recv()
        weight_pass(origin).start()
        total = total + product(turned_ref[origin], weights[origin])
        weight_all_ref[origin] = weights[origin]
    for origin in origins:
        across = origin + 1 - 2 * core
        weight_pass(across).wait_recv()
        total = total + product(turned_ref[across], weights[across])
        weight_all_ref[across] = weights[across]
    field_ref[...] = total.astype(jnp.bfloat16)

    finish_messages()
    landed[me] = message_ref[me]
    received_ref[...] = landed[...]
    for other in others:
        turned_from(other).wait_recv()
        turned_all_ref[other] = turned[other]
    for other in peers:
        weight_to(other).wait_send()
    weight_to(partner).wait_send()
    for origin in origins:
        weight_pass(origin).wait_send()
    for other in others:
        turned_to(other).wait_send()


def start_exchange(groups, shards, x_norm, head_weight, send):
    tokens, model = x_norm.shape
    devices = groups * shards
    rows = model // shards
    turned = x_norm.T.reshape(shards, rows, tokens)
    message = send.reshape(devices, send.shape[0] // devices, send.shape[1])
    in_vmem = pl.BlockSpec(memory_space=pltpu.VMEM)
    dma = pltpu.SemaphoreType.DMA
    received, turned_all, weight_all, field = pl.pallas_call(
        functools.partial(start_kernel, groups, shards),
        in_specs=[in_vmem] * 3,
        out_specs=[in_vmem] * 4,
        out_shape=[
            jax.ShapeDtypeStruct(message.shape, jnp.float32),
            jax.ShapeDtypeStruct(turned.shape, jnp.bfloat16),
            jax.ShapeDtypeStruct((shards, rows, model), jnp.bfloat16),
            jax.ShapeDtypeStruct((tokens, model), jnp.bfloat16),
        ],
        scratch_shapes=[
            pltpu.VMEM(message.shape, jnp.float32),
            pltpu.VMEM(turned.shape, jnp.bfloat16),
            pltpu.VMEM((shards, rows, model), jnp.bfloat16),
            dma((devices,)),
            dma((devices,)),
            dma((shards,)),
            dma((shards,)),
            dma((shards,)),
            dma((shards,)),
            dma((shards,)),
        ],
        compiler_params=pltpu.CompilerParams(collective_id=2, has_side_effects=True),
    )(message, turned, head_weight)
    return received.reshape(send.shape), turned_all, weight_all.reshape(model, model), field


def body(
    latents,
    head_weight,
    norm_gain,
    color_head,
    sample_points,
    sample_spacing,
    ray_targets,
    ray_scene,
):
    devices = lax.axis_size(("grp", "shard"))
    ray_count, ray_depth = sample_spacing.shape
    tokens, model = latents.shape
    field_width = color_head.shape[1]
    per_layer = field_width * field_width // model
    per_device = 4 * ray_count // devices
    slot_total = per_device * devices
    latent_f32 = latents.astype(jnp.float32)
    inv_rms = lax.rsqrt(jnp.mean(latent_f32 * latent_f32, axis=1, keepdims=True) + norm_eps)
    x_hat = latent_f32 * inv_rms
    x_norm = (x_hat * norm_gain).astype(jnp.bfloat16)
    ray_ids = jnp.arange(ray_count, dtype=jnp.int32)
    same_scene = ray_scene[:, None] == ray_scene[None, :]
    earlier = ray_ids[:, None] < ray_ids[None, :]
    ray_rank = jnp.sum(jnp.logical_and(same_scene, earlier).astype(jnp.int32), axis=0)
    slot_of_ray = ray_scene * per_device + ray_rank
    payload = jnp.concatenate(
        [sample_points, sample_spacing, ray_targets.T, jnp.ones((ray_count, 1), jnp.float32)], axis=1
    )
    send = jnp.zeros((slot_total, payload.shape[1]), jnp.float32).at[slot_of_ray].set(payload)
    received, x_turned, full_weight, field_rows = start_exchange(
        lax.axis_size("grp"), lax.axis_size("shard"), x_norm, head_weight, send
    )
    w_first = field_rows[:per_layer].reshape(field_width, field_width)
    w_second = field_rows[per_layer:].reshape(field_width, field_width)
    recv_points = received[:, : 3 * ray_depth]
    recv_spacing = received[:, 3 * ray_depth : 4 * ray_depth]
    recv_target = received[:, 4 * ray_depth : 4 * ray_depth + 3]
    recv_live = received[:, 4 * ray_depth + 3]
    scene_rays = jnp.sum(recv_live)
    scene_factor = 1.0 / (devices * scene_rays)

    slot_colors, loss_sum, grad_first, grad_second = render_slots(
        recv_points,
        recv_spacing,
        recv_target,
        recv_live * scene_factor,
        w_first,
        w_second,
        color_head,
    )
    d_field = jnp.concatenate(
        [grad_first.reshape(per_layer, model), grad_second.reshape(per_layer, model)], axis=0
    ).astype(jnp.bfloat16)
    d_norm = lax.dot_general(
        d_field,
        full_weight,
        (((1,), (1,)), ((), ())),
        preferred_element_type=jnp.float32,
    )
    gain_part = jnp.sum(d_norm * x_hat, axis=0)
    returned, loss_total, head_grad, norm_gain_grad = tail_exchange(
        lax.axis_size("grp"), lax.axis_size("shard"), x_turned, d_field, gain_part, loss_sum, slot_colors
    )
    rendered = returned[:, slot_of_ray]
    d_scaled = d_norm * norm_gain
    latent_grad = (
        inv_rms * (d_scaled - x_hat * jnp.mean(d_scaled * x_hat, axis=1, keepdims=True))
    ).astype(jnp.bfloat16)
    return (rendered, loss_total, head_grad, norm_gain_grad, latent_grad)


def solution(mesh):
    placed = (
        P(("grp", "shard"), None),
        P("shard", None),
        P(),
        P(),
        P(("grp", "shard"), None),
        P(("grp", "shard"), None),
        P(None, ("grp", "shard")),
        P(("grp", "shard")),
    )
    return jax.shard_map(
        body,
        mesh=mesh,
        in_specs=placed,
        out_specs=(
            P(None, ("grp", "shard")),
            P(),
            P("shard", None),
            P(),
            P(("grp", "shard"), None),
        ),
        check_vma=False,
    )
```

```python
import functools

import jax
import jax.numpy as jnp
from jax import lax
from jax.experimental import pallas as pl
from jax.experimental.pallas import tpu as pltpu
from jax.sharding import PartitionSpec as P

norm_eps = 1e-06


LANES = 128
HALVES = 2
SINE = (3.14159265358979, -5.16771278004997, 2.55016403987735, -0.599264529320792, 0.0821458866111282, -0.00737043094571435, 0.000466302805767613, -0.0000219153534478303)


def sine_of_pi(turns):
    whole = jnp.floor(turns + 0.5)
    rest = turns - whole
    odd = whole - 2.0 * jnp.floor(whole * 0.5)
    square = rest * rest
    value = jnp.full_like(square, SINE[-1])
    for coefficient in SINE[-2::-1]:
        value = value * square + coefficient
    return value * (rest * (1.0 - 2.0 * odd))


def ray_kernel(
    ray_depth,
    points_ref,
    spacing_ref,
    target_ref,
    factor_ref,
    first_ref,
    second_ref,
    head_ref,
    color_ref,
    loss_ref,
    d_first_ref,
    d_second_ref,
    first_t_ref,
    second_t_ref,
    grad_first_ref,
    grad_second_ref,
    raw_ref,
    draw_ref,
):
    width = second_ref.shape[0]
    fan_scale = width ** (-0.5)
    samples = points_ref.shape[1]
    chunks = samples // LANES

    @pl.when(pl.program_id(0) == 0)
    def _():
        loss_ref[...] = jnp.zeros_like(loss_ref)
        grad_first_ref[...] = jnp.zeros_like(grad_first_ref)
        grad_second_ref[...] = jnp.zeros_like(grad_second_ref)
        first_t_ref[...] = first_ref[...].T
        second_t_ref[...] = second_ref[...].T

    feature = lax.broadcasted_iota(jnp.int32, (48, 1), 0)
    component = feature % 3
    scale = jnp.exp2((feature // 6 % 8).astype(jnp.float32))
    phase = (feature // 3 % 2).astype(jnp.float32) * 0.5
    picked = jnp.where(
        component == 0,
        points_ref[0:1, :],
        jnp.where(component == 1, points_ref[1:2, :], points_ref[2:3, :]),
    )
    turns = picked * scale
    turns = turns - 2.0 * jnp.floor(turns * 0.5)
    distinct = sine_of_pi(turns + phase).astype(jnp.bfloat16)
    copies = width // 48
    h_zero = jnp.concatenate([distinct] * copies + [distinct[: width - 48 * copies]], axis=0)

    def product(a, b):
        return jnp.dot(a, b, preferred_element_type=jnp.float32)

    h_one = jnp.maximum(product(first_t_ref[...], h_zero) * fan_scale, 0.0).astype(jnp.bfloat16)
    h_two = jnp.maximum(product(second_t_ref[...], h_one) * fan_scale, 0.0).astype(jnp.bfloat16)
    raw = product(head_ref[...], h_two)
    for i in range(chunks):
        for c in range(4):
            raw_ref[c, i : i + 1, :] = raw[c : c + 1, i * LANES : (i + 1) * LANES]

    row = lax.broadcasted_iota(jnp.int32, (LANES, LANES), 0)
    column = lax.broadcasted_iota(jnp.int32, (LANES, LANES), 1)
    same = row // ray_depth == column // ray_depth
    before_sum = jnp.where(jnp.logical_and(same, row < column), 1.0, 0.0)
    behind_sum = jnp.where(jnp.logical_and(same, row > column), 1.0, 0.0)
    whole_sum = jnp.where(same, 1.0, 0.0)

    def along(values, matrix):
        return jnp.dot(
            values, matrix, preferred_element_type=jnp.float32, precision=lax.Precision.HIGHEST
        )

    spacing = spacing_ref[...]
    factor = factor_ref[...]
    density_raw = raw_ref[0]
    density = jnp.maximum(density_raw, 0.0) + jnp.log1p(jnp.exp(-jnp.abs(density_raw)))
    optical = density * spacing
    transmit = jnp.exp(-along(optical, before_sum))
    survive = jnp.exp(-optical)
    blend = transmit * (1.0 - survive)
    d_blend = jnp.zeros_like(blend)
    loss = jnp.zeros_like(blend)
    tints = []
    for c in range(3):
        albedo = 1.0 / (1.0 + jnp.exp(-raw_ref[c + 1]))
        color = along(blend * (albedo - 1.0), whole_sum) + 1.0
        color_ref[c] = color
        residual = color - target_ref[c]
        loss = loss + residual * residual
        grad_color = 2.0 * residual * factor
        d_blend = d_blend + grad_color * (albedo - 1.0)
        tints.append(grad_color * blend * albedo * (1.0 - albedo))
    loss_ref[...] += loss * factor
    behind = along(d_blend * blend, behind_sum)
    d_optical = d_blend * transmit * survive - behind
    d_density = d_optical * spacing * (1.0 / (1.0 + jnp.exp(-density_raw)))
    for c, value in enumerate([d_density] + tints):
        for i in range(chunks):
            draw_ref[c : c + 1, i * LANES : (i + 1) * LANES] = value[i : i + 1, :]
    d_raw = draw_ref[...].astype(jnp.bfloat16)
    d_htwo = lax.dot_general(
        head_ref[...], d_raw, (((0,), (0,)), ((), ())), preferred_element_type=jnp.float32
    )
    d_atwo = (jnp.where(h_two > 0, d_htwo, 0.0) * fan_scale).astype(jnp.bfloat16)
    over_samples = (((1,), (1,)), ((), ()))
    grad_second_ref[...] += lax.dot_general(
        h_one, d_atwo, over_samples, preferred_element_type=jnp.float32
    )
    d_hone = product(second_ref[...], d_atwo)
    d_aone = (jnp.where(h_one > 0, d_hone, 0.0) * fan_scale).astype(jnp.bfloat16)
    grad_first_ref[...] += lax.dot_general(
        distinct, d_aone, over_samples, preferred_element_type=jnp.float32
    )

    @pl.when(pl.program_id(0) == pl.num_programs(0) - 1)
    def _():
        first = grad_first_ref[...].astype(jnp.bfloat16)
        d_first_ref[...] = jnp.concatenate([first] * copies + [first[: width - 48 * copies]], axis=0)
        d_second_ref[...] = grad_second_ref[...].astype(jnp.bfloat16)


def render_slots(points, spacing, target, factor, w_first, w_second, color_head):
    slots, ray_depth = spacing.shape
    width = w_first.shape[0]
    total = slots * ray_depth
    block = 2048
    rows = total // LANES
    block_rows = block // LANES
    flat_points = points.reshape(slots, 3, ray_depth).transpose(1, 0, 2).reshape(3, total)
    wide_target = jnp.broadcast_to(target.T[:, :, None], (3, slots, ray_depth)).reshape(3, rows, LANES)
    wide_factor = jnp.broadcast_to(factor[:, None], (slots, ray_depth)).reshape(rows, LANES)
    fixed = lambda b: (0, 0)
    color, loss, grad_first, grad_second = pl.pallas_call(
        functools.partial(ray_kernel, ray_depth),
        grid=(total // block,),
        in_specs=[
            pl.BlockSpec((3, block), lambda b: (0, b)),
            pl.BlockSpec((block_rows, LANES), lambda b: (b, 0)),
            pl.BlockSpec((3, block_rows, LANES), lambda b: (0, b, 0)),
            pl.BlockSpec((block_rows, LANES), lambda b: (b, 0)),
            pl.BlockSpec((width, width), fixed),
            pl.BlockSpec((width, width), fixed),
            pl.BlockSpec(color_head.shape, fixed),
        ],
        out_specs=[
            pl.BlockSpec((3, block_rows, LANES), lambda b: (0, b, 0)),
            pl.BlockSpec((block_rows, LANES), fixed),
            pl.BlockSpec((width, width), fixed),
            pl.BlockSpec((width, width), fixed),
        ],
        out_shape=[
            jax.ShapeDtypeStruct((3, rows, LANES), jnp.float32),
            jax.ShapeDtypeStruct((block_rows, LANES), jnp.float32),
            jax.ShapeDtypeStruct((width, width), jnp.bfloat16),
            jax.ShapeDtypeStruct((width, width), jnp.bfloat16),
        ],
        scratch_shapes=[
            pltpu.VMEM((width, width), jnp.bfloat16),
            pltpu.VMEM((width, width), jnp.bfloat16),
            pltpu.VMEM((48, width), jnp.float32),
            pltpu.VMEM((width, width), jnp.float32),
            pltpu.VMEM((4, block_rows, LANES), jnp.float32),
            pltpu.VMEM((4, block), jnp.float32),
        ],
    )(
        flat_points,
        spacing.reshape(rows, LANES),
        wide_target,
        wide_factor,
        w_first,
        w_second,
        color_head,
    )
    colors = color.reshape(3, slots, ray_depth)[:, :, 0]
    return colors, jnp.sum(loss) * (1.0 / ray_depth), grad_first, grad_second


MESH = pl.DeviceIdType.MESH


def greet_all(groups, shards):
    me = lax.axis_index("grp") * shards + lax.axis_index("shard")
    total = groups * shards
    barrier = pltpu.get_barrier_semaphore()

    def greet(step, carry):
        other = lax.rem(me + step, total)
        pl.semaphore_signal(
            barrier, inc=1, device_id=(other // shards, lax.rem(other, shards)), device_id_type=MESH
        )
        return carry

    lax.fori_loop(1, total, greet, 0)
    pl.semaphore_wait(barrier, total - 1)


def messages(groups, shards, message_ref, landed, sent, arrived):
    me = lax.axis_index("grp") * shards + lax.axis_index("shard")
    total = groups * shards

    def copy_to(step):
        other = lax.rem(me + step, total)
        return pltpu.make_async_remote_copy(
            src_ref=message_ref.at[other],
            dst_ref=landed.at[me],
            send_sem=sent.at[other],
            recv_sem=arrived.at[me],
            device_id=(other // shards, lax.rem(other, shards)),
            device_id_type=MESH,
        )

    def copy_from(step):
        other = lax.rem(me + total - step, total)
        return pltpu.make_async_remote_copy(
            src_ref=message_ref.at[other],
            dst_ref=landed.at[other],
            send_sem=sent.at[other],
            recv_sem=arrived.at[other],
            device_id=(other // shards, lax.rem(other, shards)),
            device_id_type=MESH,
        )

    def start():
        def one(step, carry):
            copy_to(step).start()
            return carry

        lax.fori_loop(1, total, one, 0)

    def finish():
        def one(step, carry):
            copy_from(step).wait_recv()
            copy_to(step).wait_send()
            return carry

        lax.fori_loop(1, total, one, 0)

    return start, finish


def tail_kernel(
    groups,
    shards,
    message_ref,
    turned_ref,
    field_ref,
    sums_ref,
    colors_ref,
    head_ref,
    landed,
    fields,
    part,
    parts,
    done,
    message_sent,
    message_arrived,
    field_sent,
    passed_on,
    field_arrived,
    part_sent,
    part_arrived,
    done_sent,
    done_arrived,
):
    group = lax.axis_index("grp")
    shard = lax.axis_index("shard")
    me = group * shards + shard
    chips = shards // 2
    chip = shard // 2
    core = lax.rem(shard, 2)
    partner = chip * 2 + 1 - core

    def remote(source, target, send_sem, recv_sem, to_group, to_shard):
        return pltpu.make_async_remote_copy(
            src_ref=source,
            dst_ref=target,
            send_sem=send_sem,
            recv_sem=recv_sem,
            device_id=(to_group, to_shard),
            device_id_type=MESH,
        )

    width = field_ref.shape[1] // HALVES

    def columns(half):
        return pl.ds(half * width, width)

    def field_to(half, other):
        return remote(
            field_ref.at[:, columns(half)],
            fields.at[half, shard],
            field_sent.at[half, other],
            field_arrived.at[half, shard],
            group,
            other,
        )

    def field_pass(half, origin):
        return remote(
            fields.at[half, origin],
            fields.at[half, origin],
            passed_on.at[half, origin],
            field_arrived.at[half, origin],
            group,
            partner,
        )

    greet_all(groups, shards)
    start_messages, finish_messages = messages(
        groups, shards, message_ref, landed, message_sent, message_arrived
    )
    peers = [lax.rem(chip + step, chips) * 2 + core for step in range(1, chips)]
    origins = [lax.rem(chip + chips - step, chips) * 2 + core for step in range(1, chips)]
    group_steps = [lax.rem(group + step, groups) for step in range(1, groups)]
    for half in range(HALVES):
        for other in peers:
            field_to(half, other).start()
        field_to(half, partner).start()
    start_messages()

    def product(rows, field):
        return jnp.dot(rows, field, preferred_element_type=jnp.float32)

    def part_to(half, other):
        return remote(
            part.at[half, other],
            parts.at[half, group],
            part_sent.at[half, other],
            part_arrived.at[half, group],
            other,
            shard,
        )

    def part_from(half, other):
        return remote(
            part.at[half, other],
            parts.at[half, other],
            part_sent.at[half, other],
            part_arrived.at[half, other],
            other,
            shard,
        )

    def done_to(half, other):
        return remote(
            done.at[half, group],
            done.at[half, group],
            done_sent.at[half, other],
            done_arrived.at[half, group],
            other,
            shard,
        )

    def done_from(half, other):
        return remote(
            done.at[half, other],
            done.at[half, other],
            done_sent.at[half, other],
            done_arrived.at[half, other],
            other,
            shard,
        )

    def gather_half(half):
        total = product(turned_ref[shard], field_ref[:, half * width : (half + 1) * width])
        field_pass(half, partner).wait_recv()
        total = total + product(turned_ref[partner], fields[half, partner])
        for origin in origins:
            field_pass(half, origin).wait_recv()
            field_pass(half, origin).start()
            total = total + product(turned_ref[origin], fields[half, origin])
        for origin in origins:
            across = origin + 1 - 2 * core
            field_pass(half, across).wait_recv()
            total = total + product(turned_ref[across], fields[half, across])
        part[half] = total.astype(jnp.bfloat16).reshape(part.shape[1:])
        for other in group_steps:
            part_to(half, other).start()

    def sum_half(half):
        slice_sum = part[half, group].astype(jnp.float32)
        for other in group_steps:
            part_from(half, other).wait_recv()
            slice_sum = slice_sum + parts[half, other].astype(jnp.float32)
        done[half, group] = slice_sum.astype(jnp.bfloat16)
        for other in group_steps:
            done_to(half, other).start()
        head_ref[group, :, half * width : (half + 1) * width] = slice_sum

    for half in range(HALVES):
        gather_half(half)
        if half > 0:
            sum_half(half - 1)
    sum_half(HALVES - 1)

    finish_messages()
    landed[me] = message_ref[me]
    colors_ref[...] = landed[:, landed.shape[1] - 8 :, :]
    sums_ref[...] = jnp.sum(landed[...], axis=0)

    for half in range(HALVES):
        for other in group_steps:
            done_from(half, other).wait_recv()
            head_ref[other, :, half * width : (half + 1) * width] = done[half, other].astype(
                jnp.float32
            )
        for other in peers:
            field_to(half, other).wait_send()
        field_to(half, partner).wait_send()
        for origin in origins:
            field_pass(half, origin).wait_send()
        for other in group_steps:
            part_to(half, other).wait_send()
            done_to(half, other).wait_send()


def tail_exchange(groups, shards, turned, d_field, gain_part, loss_sum, slot_colors):
    tokens, model = d_field.shape
    devices = groups * shards
    rows = model // shards
    gain_rows = model // LANES
    per_device = slot_colors.shape[1] // devices
    shared = jnp.concatenate(
        [gain_part.reshape(gain_rows, LANES), jnp.broadcast_to(loss_sum, (1, LANES))], axis=0
    )
    own = jnp.pad(
        slot_colors.reshape(3, devices, per_device).transpose(1, 0, 2),
        ((0, 0), (0, 4), (0, LANES - per_device)),
    )
    message = jnp.concatenate(
        [jnp.broadcast_to(shared[None], (devices,) + shared.shape), own], axis=1
    )
    in_vmem = pl.BlockSpec(memory_space=pltpu.VMEM)
    dma = pltpu.SemaphoreType.DMA
    sums, colors, head = pl.pallas_call(
        functools.partial(tail_kernel, groups, shards),
        in_specs=[in_vmem] * 3,
        out_specs=[in_vmem] * 3,
        out_shape=[
            jax.ShapeDtypeStruct(message.shape[1:], jnp.float32),
            jax.ShapeDtypeStruct((devices, 8, LANES), jnp.float32),
            jax.ShapeDtypeStruct((groups, rows // groups, model), jnp.float32),
        ],
        scratch_shapes=[
            pltpu.VMEM(message.shape, jnp.float32),
            pltpu.VMEM((HALVES, shards, tokens, model // HALVES), jnp.bfloat16),
            pltpu.VMEM((HALVES, groups, rows // groups, model // HALVES), jnp.bfloat16),
            pltpu.VMEM((HALVES, groups, rows // groups, model // HALVES), jnp.bfloat16),
            pltpu.VMEM((HALVES, groups, rows // groups, model // HALVES), jnp.bfloat16),
            dma((devices,)),
            dma((devices,)),
            dma((HALVES, shards)),
            dma((HALVES, shards)),
            dma((HALVES, shards)),
            dma((HALVES, groups)),
            dma((HALVES, groups)),
            dma((HALVES, groups)),
            dma((HALVES, groups)),
        ],
        compiler_params=pltpu.CompilerParams(collective_id=1, has_side_effects=True),
    )(message, turned, d_field)
    gain = sums[:gain_rows].reshape(model)
    loss = sums[gain_rows, 0]
    returned = colors[:, 1:4, :per_device].transpose(1, 0, 2).reshape(3, devices * per_device)
    return returned, loss, head.reshape(rows, model), gain


def start_kernel(
    groups,
    shards,
    message_ref,
    turned_ref,
    weight_ref,
    received_ref,
    turned_all_ref,
    weight_all_ref,
    field_ref,
    landed,
    turned,
    weights,
    message_sent,
    message_arrived,
    turned_sent,
    turned_arrived,
    weight_sent,
    passed_on,
    weight_arrived,
):
    group = lax.axis_index("grp")
    shard = lax.axis_index("shard")
    me = group * shards + shard
    chips = shards // 2
    chip = shard // 2
    core = lax.rem(shard, 2)
    partner = chip * 2 + 1 - core

    def remote(source, target, send_sem, recv_sem, to_shard):
        return pltpu.make_async_remote_copy(
            src_ref=source,
            dst_ref=target,
            send_sem=send_sem,
            recv_sem=recv_sem,
            device_id=(group, to_shard),
            device_id_type=MESH,
        )

    def weight_to(other):
        return remote(
            weight_ref, weights.at[shard], weight_sent.at[other], weight_arrived.at[shard], other
        )

    def weight_pass(origin):
        return remote(
            weights.at[origin],
            weights.at[origin],
            passed_on.at[origin],
            weight_arrived.at[origin],
            partner,
        )

    def turned_to(other):
        return remote(
            turned_ref.at[other],
            turned.at[shard],
            turned_sent.at[other],
            turned_arrived.at[shard],
            other,
        )

    def turned_from(other):
        return remote(
            turned_ref.at[other],
            turned.at[other],
            turned_sent.at[other],
            turned_arrived.at[other],
            other,
        )

    greet_all(groups, shards)
    start_messages, finish_messages = messages(
        groups, shards, message_ref, landed, message_sent, message_arrived
    )
    peers = [lax.rem(chip + step, chips) * 2 + core for step in range(1, chips)]
    origins = [lax.rem(chip + chips - step, chips) * 2 + core for step in range(1, chips)]
    others = [lax.rem(shard + step, shards) for step in range(1, shards)]
    for other in peers:
        weight_to(other).start()
    weight_to(partner).start()
    start_messages()
    for other in others:
        turned_to(other).start()

    def product(rows, weight):
        return lax.dot_general(
            rows, weight, (((0,), (0,)), ((), ())), preferred_element_type=jnp.float32
        )

    total = product(turned_ref[shard], weight_ref[...])
    weight_all_ref[shard] = weight_ref[...]
    turned_all_ref[shard] = turned_ref[shard]
    weight_pass(partner).wait_recv()
    total = total + product(turned_ref[partner], weights[partner])
    weight_all_ref[partner] = weights[partner]
    for origin in origins:
        weight_pass(origin).wait_recv()
        weight_pass(origin).start()
        total = total + product(turned_ref[origin], weights[origin])
        weight_all_ref[origin] = weights[origin]
    for origin in origins:
        across = origin + 1 - 2 * core
        weight_pass(across).wait_recv()
        total = total + product(turned_ref[across], weights[across])
        weight_all_ref[across] = weights[across]
    field_ref[...] = total.astype(jnp.bfloat16)

    finish_messages()
    landed[me] = message_ref[me]
    received_ref[...] = landed[...]
    for other in others:
        turned_from(other).wait_recv()
        turned_all_ref[other] = turned[other]
    for other in peers:
        weight_to(other).wait_send()
    weight_to(partner).wait_send()
    for origin in origins:
        weight_pass(origin).wait_send()
    for other in others:
        turned_to(other).wait_send()


def start_exchange(groups, shards, x_norm, head_weight, send):
    tokens, model = x_norm.shape
    devices = groups * shards
    rows = model // shards
    turned = x_norm.T.reshape(shards, rows, tokens)
    message = send.reshape(devices, send.shape[0] // devices, send.shape[1])
    in_vmem = pl.BlockSpec(memory_space=pltpu.VMEM)
    dma = pltpu.SemaphoreType.DMA
    received, turned_all, weight_all, field = pl.pallas_call(
        functools.partial(start_kernel, groups, shards),
        in_specs=[in_vmem] * 3,
        out_specs=[in_vmem] * 4,
        out_shape=[
            jax.ShapeDtypeStruct(message.shape, jnp.float32),
            jax.ShapeDtypeStruct(turned.shape, jnp.bfloat16),
            jax.ShapeDtypeStruct((shards, rows, model), jnp.bfloat16),
            jax.ShapeDtypeStruct((tokens, model), jnp.bfloat16),
        ],
        scratch_shapes=[
            pltpu.VMEM(message.shape, jnp.float32),
            pltpu.VMEM(turned.shape, jnp.bfloat16),
            pltpu.VMEM((shards, rows, model), jnp.bfloat16),
            dma((devices,)),
            dma((devices,)),
            dma((shards,)),
            dma((shards,)),
            dma((shards,)),
            dma((shards,)),
            dma((shards,)),
        ],
        compiler_params=pltpu.CompilerParams(collective_id=2, has_side_effects=True),
    )(message, turned, head_weight)
    return received.reshape(send.shape), turned_all, weight_all.reshape(model, model), field


def body(
    latents,
    head_weight,
    norm_gain,
    color_head,
    sample_points,
    sample_spacing,
    ray_targets,
    ray_scene,
):
    devices = lax.axis_size(("grp", "shard"))
    ray_count, ray_depth = sample_spacing.shape
    tokens, model = latents.shape
    field_width = color_head.shape[1]
    per_layer = field_width * field_width // model
    per_device = 4 * ray_count // devices
    slot_total = per_device * devices
    latent_f32 = latents.astype(jnp.float32)
    inv_rms = lax.rsqrt(jnp.mean(latent_f32 * latent_f32, axis=1, keepdims=True) + norm_eps)
    x_hat = latent_f32 * inv_rms
    x_norm = (x_hat * norm_gain).astype(jnp.bfloat16)
    ray_ids = jnp.arange(ray_count, dtype=jnp.int32)
    same_scene = ray_scene[:, None] == ray_scene[None, :]
    earlier = ray_ids[:, None] < ray_ids[None, :]
    ray_rank = jnp.sum(jnp.logical_and(same_scene, earlier).astype(jnp.int32), axis=0)
    slot_of_ray = ray_scene * per_device + ray_rank
    payload = jnp.concatenate(
        [sample_points, sample_spacing, ray_targets.T, jnp.ones((ray_count, 1), jnp.float32)], axis=1
    )
    send = jnp.zeros((slot_total, payload.shape[1]), jnp.float32).at[slot_of_ray].set(payload)
    received, x_turned, full_weight, field_rows = start_exchange(
        lax.axis_size("grp"), lax.axis_size("shard"), x_norm, head_weight, send
    )
    w_first = field_rows[:per_layer].reshape(field_width, field_width)
    w_second = field_rows[per_layer:].reshape(field_width, field_width)
    recv_points = received[:, : 3 * ray_depth]
    recv_spacing = received[:, 3 * ray_depth : 4 * ray_depth]
    recv_target = received[:, 4 * ray_depth : 4 * ray_depth + 3]
    recv_live = received[:, 4 * ray_depth + 3]
    scene_rays = jnp.sum(recv_live)
    scene_factor = 1.0 / (devices * scene_rays)

    slot_colors, loss_sum, grad_first, grad_second = render_slots(
        recv_points,
        recv_spacing,
        recv_target,
        recv_live * scene_factor,
        w_first,
        w_second,
        color_head,
    )
    d_field = jnp.concatenate(
        [grad_first.reshape(per_layer, model), grad_second.reshape(per_layer, model)], axis=0
    )
    d_norm = lax.dot_general(
        d_field,
        full_weight,
        (((1,), (1,)), ((), ())),
        preferred_element_type=jnp.float32,
    )
    gain_part = jnp.sum(d_norm * x_hat, axis=0)
    returned, loss_total, head_grad, norm_gain_grad = tail_exchange(
        lax.axis_size("grp"), lax.axis_size("shard"), x_turned, d_field, gain_part, loss_sum, slot_colors
    )
    rendered = returned[:, slot_of_ray]
    d_scaled = d_norm * norm_gain
    latent_grad = (
        inv_rms * (d_scaled - x_hat * jnp.mean(d_scaled * x_hat, axis=1, keepdims=True))
    ).astype(jnp.bfloat16)
    return (rendered, loss_total, head_grad, norm_gain_grad, latent_grad)


def solution(mesh):
    placed = (
        P(("grp", "shard"), None),
        P("shard", None),
        P(),
        P(),
        P(("grp", "shard"), None),
        P(("grp", "shard"), None),
        P(None, ("grp", "shard")),
        P(("grp", "shard")),
    )
    return jax.shard_map(
        body,
        mesh=mesh,
        in_specs=placed,
        out_specs=(
            P(None, ("grp", "shard")),
            P(),
            P("shard", None),
            P(),
            P(("grp", "shard"), None),
        ),
        check_vma=False,
    )
```
